32 devices in a mesh: tm: 8 (over y, x, core), fsdp: 4 (over z).
Axes of the slice: x: 2, y: 2, z: 4, core: 2. Of those that a mesh axis runs over, the one named last changes fastest.
Arguments:
- frames: bfloat16 [4, 1024, 1024], P('fsdp', 'tm'), may hold values from -6 to 6
- gain_one: float32 [1024], replicated, may hold values from 0.1 to 1.9
- qkv_one: bfloat16 [1024, 3072], P('fsdp'), may hold values from -0.1875 to 0.1875
- out_one: bfloat16 [1024, 1024], P('fsdp'), may hold values from -0.1875 to 0.1875
- gain_two: float32 [1024], replicated, may hold values from 0.1 to 1.9
- qkv_two: bfloat16 [1024, 3072], P('fsdp'), may hold values from -0.1875 to 0.1875
- lengths: int32 [4], P('fsdp'), may hold values from 512 to 1024, as said below
- left_counts: int32 [4], P('fsdp'), may hold values from 0 to 2, as said below
- cotangent: bfloat16 [4, 1024, 1024], P('fsdp', 'tm'), may hold values from -6 to 6
Outputs:
- context: bfloat16 [4, 1024, 1024], P('fsdp', 'tm')
- weight_grad: float32 [1024, 1024], P(('tm', 'fsdp'))
The draws below stay inside these ranges and needn't reach their ends.
Inputs may be any that keep to these rules, and one draw needn't show every extreme that they name: `lengths`: some utterance is complete in every draw. `left_counts`: in every draw some utterance takes 2 blocks and another none.
All inputs are finite; a program needn't handle non-finite values.
Results may differ from the reference program's by a relative error of at most 0.029.
Values may be sent and summed in bfloat16 or wider, within the bound.
A program may use at most 64 MiB of HBM per device.

```python
import jax
import jax.numpy as jnp
from jax import lax

D = 1024
HEADS = 16
HEAD = 64
FR = 128
LEFT_MAX = 2
RIGHT = 23
UTTS = 4
FRAMES = 1024
N_TM = 8


def draw_frames(key, part):
    noise = jax.random.truncated_normal(jax.random.fold_in(key, 31), -6.0, 6.0, (UTTS, FRAMES, D), jnp.float32)
    return noise.astype(jnp.bfloat16)


def projection_draw(key, salt):
    scale = D ** (-0.5)
    base = jax.random.truncated_normal(jax.random.fold_in(key, salt), -6.0, 6.0, (D, 3 * D), jnp.float32) * scale
    return base.astype(jnp.bfloat16)


def draw_qkv_one(key, part):
    return projection_draw(key, 41)


def draw_qkv_two(key, part):
    return projection_draw(key, 51)


def draw_lengths(key, part):
    first = jax.random.fold_in(key, 11)
    second = jax.random.fold_in(key, 12)
    values = jax.random.randint(first, (UTTS,), FRAMES // 2, FRAMES + 1, dtype=jnp.int32)
    chosen = jax.random.randint(second, (), 0, UTTS, dtype=jnp.int32)
    return jnp.where(jnp.arange(UTTS, dtype=jnp.int32) == chosen, FRAMES, values).astype(jnp.int32)


def draw_left_counts(key, part):
    first = jax.random.fold_in(key, 21)
    second = jax.random.fold_in(key, 22)
    third = jax.random.fold_in(key, 23)
    values = jax.random.randint(first, (UTTS,), 0, LEFT_MAX + 1, dtype=jnp.int32)
    chosen = jax.random.randint(second, (), 0, UTTS, dtype=jnp.int32)
    offset = jax.random.randint(third, (), 1, UTTS, dtype=jnp.int32)
    other = (chosen + offset) % UTTS
    index = jnp.arange(UTTS, dtype=jnp.int32)
    values = jnp.where(index == chosen, LEFT_MAX, values)
    values = jnp.where(index == other, 0, values)
    return values.astype(jnp.int32)


def with_spikes(entries, own_key, source, target, parts, factor):
    def block_of(axis_at):
        return (jnp.arange(entries.shape[axis_at]) // (entries.shape[axis_at] // parts)).reshape((-1,) + (1,) * (entries.ndim - 1 - axis_at))

    near = jax.random.permutation(own_key, parts)[block_of(target)]
    other_side = (block_of(target) + parts // 2) % parts
    return jnp.where((block_of(source) == near) | (block_of(source) == other_side), factor * entries, entries)


def block_levels(stream_key, shape, shards, smallest, high):
    loudness, own = 1.0, jax.random.fold_in(stream_key, 6)
    for dim, blocks in shards:
        heights = jnp.exp(jax.random.uniform(jax.random.fold_in(own, dim), (blocks,), jnp.float32, smallest / len(shards), high / len(shards)))
        loudness = loudness * jnp.repeat(heights, shape[dim] // blocks).reshape([-1 if axis == dim else 1 for axis in range(len(shape))])
    return loudness


def gaussian(rng, shape, spread, limit, shards=(), kind=jnp.bfloat16):
    values = spread * jax.random.normal(rng, shape, jnp.float32)
    if shards:
        values = values * block_levels(rng, shape, shards, -0.22, 0.18)
    return jnp.clip(values, -limit, limit).astype(kind)


def bell_draw_with(stream_key, dims, scale, bound, shards, heavy, held_as=jnp.bfloat16):
    result = scale * jax.random.normal(stream_key, dims, jnp.float32)
    if shards:
        result = result * block_levels(stream_key, dims, shards, -0.22, 0.18)
    return jnp.clip(with_spikes(result, jax.random.fold_in(stream_key, 3), *heavy), -bound, bound).astype(held_as)


def setup_inputs(seed: int = 0) -> dict:
    key_of = jax.random.split(jax.random.key(seed), 10)
    frames = draw_frames(jax.random.fold_in(key_of[9], 71), 0)
    gain_one = jnp.clip(1.0 + 0.18 * jax.random.normal(key_of[1], (D,), jnp.float32), 0.1, 1.9)
    qkv_one = draw_qkv_one(jax.random.fold_in(key_of[9], 71), 0)
    out_one = gaussian(key_of[3], (D, D), D ** -0.5, 0.1875, ((0, 4),))
    gain_two = jnp.clip(1.0 + 0.18 * jax.random.normal(key_of[4], (D,), jnp.float32), 0.1, 1.9)
    qkv_two = draw_qkv_two(jax.random.fold_in(key_of[9], 71), 0)
    lengths = draw_lengths(jax.random.fold_in(key_of[9], 71), 0)
    left_counts = draw_left_counts(jax.random.fold_in(key_of[9], 71), 0)
    cotangent = bell_draw_with(key_of[8], (UTTS, FRAMES, D), 1.0, 6.0, ((0, 4), (1, 8)), (1, 2, 8, 2.0))
    return dict(frames=frames, gain_one=gain_one, qkv_one=qkv_one, out_one=out_one, gain_two=gain_two, qkv_two=qkv_two, lengths=lengths, left_counts=left_counts, cotangent=cotangent)


def norm_rows(values, gain):
    wide = values.astype(jnp.float32)
    mean = lax.optimization_barrier(jnp.mean(wide, axis=-1, keepdims=True))
    var = lax.optimization_barrier(jnp.mean((wide - mean) ** 2, axis=-1, keepdims=True))
    return ((wide - mean) * lax.rsqrt(var + 1e-05) * gain.astype(jnp.float32)).astype(jnp.bfloat16)

def attend(query, keys, values, allowed):
    scale = 1.0 / HEAD ** 0.5
    scores = jnp.einsum('qhe,khe->hqk', query.astype(jnp.float32), keys.astype(jnp.float32)) * scale
    scores = jnp.where(allowed[None], scores, -1e+30)
    top = lax.optimization_barrier(jnp.max(scores, axis=-1, keepdims=True))
    expo = jnp.exp(scores - top)
    weights = (expo / lax.optimization_barrier(jnp.sum(expo, axis=-1, keepdims=True))).astype(jnp.bfloat16)
    ctx = jnp.einsum('hqk,khe->qhe', weights.astype(jnp.float32), values.astype(jnp.float32))
    return ctx.reshape(query.shape[0], D).astype(jnp.bfloat16)

def one_utterance(frames_u, gain_one, qkv_one, out_one, gain_two, qkv_two, length, count):
    norm_one = norm_rows(frames_u, gain_one)
    proj = jnp.dot(norm_one, qkv_one, preferred_element_type=jnp.float32).astype(jnp.bfloat16)
    query = proj[:, :D].reshape(FRAMES, HEADS, HEAD)
    keys = proj[:, D:2 * D].reshape(FRAMES, HEADS, HEAD)
    values = proj[:, 2 * D:].reshape(FRAMES, HEADS, HEAD)
    lead = jnp.zeros((LEFT_MAX * FR, HEADS, HEAD), jnp.bfloat16)
    keys_pad = jnp.concatenate([lead, keys], axis=0)
    values_pad = jnp.concatenate([lead, values], axis=0)
    rows = jnp.arange(FR, dtype=jnp.int32)
    cols = jnp.arange((LEFT_MAX + 1) * FR, dtype=jnp.int32)

    def causal_block(block):
        start = (block * FR).astype(jnp.int32)
        qblock = lax.dynamic_slice_in_dim(query, start, FR, 0)
        kblock = lax.dynamic_slice_in_dim(keys_pad, start, (LEFT_MAX + 1) * FR, 0)
        vblock = lax.dynamic_slice_in_dim(values_pad, start, (LEFT_MAX + 1) * FR, 0)
        tpos = block * FR + rows[:, None]
        spos = (block - LEFT_MAX) * FR + cols[None, :]
        apart = LEFT_MAX - cols[None, :] // FR
        allowed = (spos >= 0) & (spos <= tpos) & (apart <= count) & ((spos < length) | (spos == tpos))
        return attend(qblock, kblock, vblock, allowed)
    ctx_one = lax.map(causal_block, jnp.arange(N_TM, dtype=jnp.int32)).reshape(FRAMES, D)
    hidden = (frames_u.astype(jnp.float32) + jnp.dot(ctx_one, out_one, preferred_element_type=jnp.float32)).astype(jnp.bfloat16)
    norm_two = norm_rows(hidden, gain_two)
    proj2 = jnp.dot(norm_two, qkv_two, preferred_element_type=jnp.float32).astype(jnp.bfloat16)
    query2 = proj2[:, :D].reshape(FRAMES, HEADS, HEAD)
    tail = jnp.zeros((FR, HEADS, HEAD), jnp.bfloat16)
    keys2 = jnp.concatenate([proj2[:, D:2 * D].reshape(FRAMES, HEADS, HEAD), tail], axis=0)
    values2 = jnp.concatenate([proj2[:, 2 * D:].reshape(FRAMES, HEADS, HEAD), tail], axis=0)
    cols2 = jnp.arange(FR + RIGHT, dtype=jnp.int32)

    def ahead_block(block):
        start = (block * FR).astype(jnp.int32)
        qblock = lax.dynamic_slice_in_dim(query2, start, FR, 0)
        kblock = lax.dynamic_slice_in_dim(keys2, start, FR + RIGHT, 0)
        vblock = lax.dynamic_slice_in_dim(values2, start, FR + RIGHT, 0)
        tpos = block * FR + rows[:, None]
        spos = block * FR + cols2[None, :]
        allowed = (cols2[None, :] <= rows[:, None] + RIGHT) & ((spos < length) | (spos == tpos))
        ctx = attend(qblock, kblock, vblock, allowed)
        valid = block * FR + rows < length
        return jnp.where(valid[:, None], ctx, jnp.zeros_like(ctx))
    return lax.map(ahead_block, jnp.arange(N_TM, dtype=jnp.int32)).reshape(FRAMES, D)

def reference(frames, gain_one, qkv_one, out_one, gain_two, qkv_two, lengths, left_counts, cotangent):

    def per_utt(index):
        return one_utterance(frames[index], gain_one, qkv_one, out_one, gain_two, qkv_two, lengths[index], left_counts[index])
    context = lax.map(per_utt, jnp.arange(UTTS, dtype=jnp.int32))
    weight_grad = jnp.dot(cotangent.reshape(-1, D).T, context.reshape(-1, D), preferred_element_type=jnp.float32)
    return (context, weight_grad)
```

```python
import functools

import jax
import jax.numpy as jnp
from jax import lax
from jax.experimental import pallas as pl
from jax.experimental.pallas import tpu as pltpu
from jax.sharding import PartitionSpec as P

HEADS = 16
LEFT_MAX = 2
RIGHT = 23


def from_behind(block, axis, distance):
    devices = range(lax.axis_size(axis))
    route = [(i - distance, i) for i in devices if i - distance in devices]
    return lax.ppermute(block, axis, route)


def norm_rows(values, gain):
    wide = values.astype(jnp.float32)
    mean = jnp.mean(wide, axis=-1, keepdims=True)
    var = jnp.mean((wide - mean) ** 2, axis=-1, keepdims=True)
    return ((wide - mean) * lax.rsqrt(var + 1e-05) * gain).astype(jnp.bfloat16)


def attend(query, keys, values, allowed, heads):
    rows_q, width = query.shape
    head = width // heads
    scale = 1.0 / head**0.5
    q_heads = query.reshape(rows_q, heads, head)
    k_heads = keys.reshape(keys.shape[0], heads, head)
    v_heads = values.reshape(values.shape[0], heads, head)
    scores = (
        jnp.einsum("qhe,khe->hqk", q_heads, k_heads, preferred_element_type=jnp.float32) * scale
    )
    scores = jnp.where(allowed[None], scores, -1e30)
    top = jnp.max(scores, axis=-1, keepdims=True)
    expo = jnp.exp(scores - top)
    weights = (expo / jnp.sum(expo, axis=-1, keepdims=True)).astype(jnp.bfloat16)
    ctx = jnp.einsum("hqk,khe->qhe", weights, v_heads, preferred_element_type=jnp.float32)
    return ctx.reshape(rows_q, width).astype(jnp.bfloat16)


def add_rows(left, piece):
    return jnp.dot(left, piece, preferred_element_type=jnp.float32)


def on_device(
    frames, gain_one, qkv_one, out_one, gain_two, qkv_two, lengths, left_counts, cotangent
):
    local = frames[0]
    grad_in = cotangent[0]
    fr, width = local.shape
    block = lax.axis_index("tm")
    length = lengths[0]
    count = left_counts[0]
    norm_one = norm_rows(local, gain_one)
    proj = add_rows(norm_one, lax.all_gather(qkv_one, "fsdp", axis=0, tiled=True))
    proj = proj.astype(jnp.bfloat16)
    query = proj[:, :width]
    key_value = proj[:, width:]
    earlier = [from_behind(key_value, "tm", step) for step in range(LEFT_MAX, 0, -1)]
    gathered = jnp.concatenate(earlier + [key_value], axis=0)
    rows = jnp.arange(fr, dtype=jnp.int32)
    cols = jnp.arange((LEFT_MAX + 1) * fr, dtype=jnp.int32)
    tpos = block * fr + rows[:, None]
    spos = (block - LEFT_MAX) * fr + cols[None, :]
    apart = LEFT_MAX - cols[None, :] // fr
    allowed = (spos >= 0) & (spos <= tpos) & (apart <= count) & ((spos < length) | (spos == tpos))
    ctx_one = attend(query, gathered[:, :width], gathered[:, width:], allowed, HEADS)
    out_proj = add_rows(ctx_one, lax.all_gather(out_one, "fsdp", axis=0, tiled=True))
    hidden = (local.astype(jnp.float32) + out_proj).astype(jnp.bfloat16)
    norm_two = norm_rows(hidden, gain_two)
    proj2 = add_rows(norm_two, lax.all_gather(qkv_two, "fsdp", axis=0, tiled=True))
    proj2 = proj2.astype(jnp.bfloat16)
    query2 = proj2[:, :width]
    key_value2 = proj2[:, width:]
    ahead = from_behind(key_value2[:RIGHT], "tm", -1)
    joined = jnp.concatenate([key_value2, ahead], axis=0)
    cols2 = jnp.arange(fr + RIGHT, dtype=jnp.int32)
    spos2 = block * fr + cols2[None, :]
    allowed2 = (cols2[None, :] <= rows[:, None] + RIGHT) & ((spos2 < length) | (spos2 == tpos))
    ctx_two = attend(query2, joined[:, :width], joined[:, width:], allowed2, HEADS)
    valid = block * fr + rows < length
    context = jnp.where(valid[:, None], ctx_two, jnp.zeros_like(ctx_two))
    weight_grad = lax.psum_scatter(
        lax.dot_general(
            grad_in, context, (((0,), (0,)), ((), ())), preferred_element_type=jnp.float32
        ),
        ("tm", "fsdp"),
        scatter_dimension=0,
        tiled=True,
    )
    return (context[None], weight_grad)


MESH = pl.DeviceIdType.MESH


def flip(index, mask):
    out, bit = index, 1
    while bit <= mask:
        if mask & bit:
            out = out + bit * (1 - 2 * ((index // bit) % 2))
        bit *= 2
    return out


def heads_kernel(
    n,
    nz,
    frames_ref, gain_one_ref, qkv_one_ref, out_one_ref, gain_two_ref, qkv_two_ref,
    length_ref, count_ref, cot_ref,
    context_ref, grad_ref,
    nbuf, nbuf2, w1, w2, wo, cotv, cott, q1, k1, v1, ctx1s, ctx1, q2, k2, v2, ctx2s, ctx2,
    gsend, grecv, gsum, wgr,
    local_sem, ag_send, ag_recv, ch_send, ch_recv, a2_send, a2_recv, z_send, z_recv,
):
    t = lax.axis_index("tm")
    z = lax.axis_index("fsdp")
    fr, width = frames_ref.shape
    cols = width // n
    head = width // HEADS
    per = HEADS // n
    rows = width // nz
    part = rows // n
    scale = 1.0 / head**0.5
    mine = pl.multiple_of(t * cols, cols)
    chips = n // 2

    def at_cols(index):
        return pl.ds(pl.multiple_of(index * cols, cols), cols)

    def at_rows(index, size):
        return pl.ds(pl.multiple_of(index * size, size), size)

    own_rows = at_rows(z, rows)
    local = []
    for j in range(3):
        for which, (src, dst) in enumerate(((qkv_one_ref, w1), (qkv_two_ref, w2))):
            local.append(
                pltpu.make_async_copy(
                    src.at[:, pl.ds(pl.multiple_of(j * width + mine, cols), cols)],
                    dst.at[own_rows, pl.ds(j * cols, cols)],
                    local_sem.at[2 * j + which],
                )
            )
    local.append(
        pltpu.make_async_copy(
            out_one_ref.at[:, pl.ds(mine, cols)], wo.at[own_rows, pl.ds(mine, cols)], local_sem.at[6]
        )
    )
    local.append(pltpu.make_async_copy(cot_ref, cotv, local_sem.at[7]))
    for copy in (local[0], local[2], local[4], local[6], local[7], local[1], local[3], local[5]):
        copy.start()

    barrier = pltpu.get_barrier_semaphore()
    for d in range(1, n):
        pl.semaphore_signal(
            barrier, inc=1, device_id=(lax.rem(t + d, n), z), device_id_type=MESH
        )
    for d in range(1, nz):
        pl.semaphore_signal(
            barrier, inc=1, device_id=(t, lax.rem(z + d, nz)), device_id_type=MESH
        )
    pl.semaphore_wait(barrier, n + nz - 2)

    half = rows // 2

    def chain_view(which, shard, h):
        span = pl.ds(pl.multiple_of(shard * rows + h * half, half), half)
        if which == 1:
            return wo.at[span, pl.ds(mine, cols)]
        return (w1, None, w2)[which].at[span, :]

    def chain_copy(which, step, up, h):
        shard = z - step if up else z + step
        shard = jnp.clip(shard, 0, nz - 1)
        to = jnp.clip(z + 1 if up else z - 1, 0, nz - 1)
        view = chain_view(which, shard, h)
        return pltpu.make_async_remote_copy(
            src_ref=view,
            dst_ref=view,
            send_sem=ch_send.at[which, 0 if up else 1, step, h],
            recv_sem=ch_recv.at[which, shard, h],
            device_id=(t, to),
            device_id_type=MESH,
        )

    def chain_cond(step, up):
        if up:
            return (z >= step) & (z < nz - 1)
        return (z + step < nz) & (z > 0)

    def chain(which, step):
        for h in range(2):
            for up in (True, False):
                @pl.when(chain_cond(step, up))
                def _():
                    copy = chain_copy(which, step, up, h)
                    if step:
                        copy.wait_recv()
                    copy.start()

    def chain_end(which):
        for edge, up in ((nz - 1, True), (0, False)):
            @pl.when(z == edge)
            def _():
                for step in range(1, nz):
                    for h in range(2):
                        shard = edge - step if up else edge + step
                        view = chain_view(which, shard, h)
                        pltpu.make_async_remote_copy(
                            src_ref=view,
                            dst_ref=view,
                            send_sem=ch_send.at[which, 0, 0, h],
                            recv_sem=ch_recv.at[which, shard, h],
                            device_id=(t, edge - 1 if up else edge + 1),
                            device_id_type=MESH,
                        ).wait_recv()

    def chain_sent(which):
        for step in range(nz - 1):
            for up in (True, False):
                for h in range(2):
                    @pl.when(chain_cond(step, up))
                    def _():
                        chain_copy(which, step, up, h).wait_send()

    def ag_view(which, index):
        if which == 0:
            return nbuf.at[index]
        if which == 1:
            return cott.at[:, at_cols(index)]
        if which == 2:
            return wo.at[:, at_cols(index)]
        return nbuf2.at[index]

    def ag_copy(which, slot):
        if slot == 0:
            block, to = t, flip(t, 1)
        elif slot < chips:
            block, to = t, flip(t, 2 * slot)
        else:
            block, to = flip(t, 2 * (slot - chips + 1)), flip(t, 1)
        view = ag_view(which, block)
        return pltpu.make_async_remote_copy(
            src_ref=view, dst_ref=view,
            send_sem=ag_send.at[which, slot], recv_sem=ag_recv.at[which, slot],
            device_id=(to, z), device_id_type=MESH,
        )

    def ag_wait(which, slot):
        if slot == 0:
            block = flip(t, 1)
        elif slot < chips:
            block = flip(t, 2 * slot)
        else:
            block = flip(t, 2 * (slot - chips + 1) + 1)
        view = ag_view(which, block)
        pltpu.make_async_remote_copy(
            src_ref=view, dst_ref=view,
            send_sem=ag_send.at[which, slot], recv_sem=ag_recv.at[which, slot],
            device_id=(flip(t, 1), z), device_id_type=MESH,
        ).wait_recv()

    def ag_start(which):
        for slot in list(range(1, chips)) + [0]:
            ag_copy(which, slot).start()

    def ag_forward(which):
        for j in range(1, chips):
            ag_wait(which, j)
            ag_copy(which, chips + j - 1).start()

    def ag_sent(which):
        for slot in range(2 * chips - 1):
            ag_copy(which, slot).wait_send()

    for j in (0, 2, 4):
        local[j].wait()
    chain(0, 0)
    nbuf[t] = norm_rows(frames_ref[...], gain_one_ref[...])
    ag_start(0)
    local[6].wait()
    local[7].wait()
    turned = cotv[...].T
    for zz in range(nz):
        for tt in range(n):
            cott[zz * rows + tt * part : zz * rows + (tt + 1) * part, pl.ds(mine, cols)] = turned[
                (tt * nz + zz) * part : (tt * nz + zz + 1) * part
            ]
    lead = LEFT_MAX * fr
    zeros = jnp.zeros((lead, cols), jnp.bfloat16)
    k1[0:lead, :] = zeros
    v1[0:lead, :] = zeros
    k2[n * fr :, :] = zeros[:fr]
    v2[n * fr :, :] = zeros[:fr]
    for step in range(1, nz - 1):
        chain(0, step)
        chain(1, step - 1)
    ag_forward(0)
    ag_start(1)
    chain(1, nz - 2)
    for j in (1, 3, 5):
        local[j].wait()
    chain(2, 0)

    def project(buf, weight, q, k, v, before, pair):
        left = buf[pl.ds(pair * 2, 2)].reshape(2 * fr, width)
        out = jnp.dot(left, weight[...], preferred_element_type=jnp.float32).astype(jnp.bfloat16)
        span = at_rows(pair, 2 * fr)
        q[span, :] = out[:, :cols]
        after = pl.ds(pl.multiple_of(pair * 2 * fr + before, fr), 2 * fr)
        k[after, :] = out[:, cols : 2 * cols]
        v[after, :] = out[:, 2 * cols :]

    chain_end(0)
    ag_wait(0, 0)
    project(nbuf, w1, q1, k1, v1, lead, t // 2)
    for j in range(1, chips):
        ag_wait(0, chips + j - 1)
        project(nbuf, w1, q1, k1, v1, lead, flip(t, 2 * j) // 2)
    chain_end(1)

    length = length_ref[0]
    count = count_ref[0]

    def attend_block(query, keys, values, allowed):
        lane = lax.broadcasted_iota(jnp.int32, (fr, cols), 1) // head
        blank = jnp.zeros_like(query)
        stacked = jnp.concatenate([jnp.where(lane == h, query, blank) for h in range(per)], axis=0)
        scores = lax.dot_general(
            stacked, keys, (((1,), (1,)), ((), ())), preferred_element_type=jnp.float32
        ) * scale
        scores = scores.reshape(per, fr, keys.shape[0])
        scores = jnp.where(allowed[None], scores, -1e30)
        top = jnp.max(scores, axis=-1, keepdims=True)
        expo = jnp.exp(scores - top)
        weights = expo * (1.0 / jnp.sum(expo, axis=-1, keepdims=True))
        weights = weights.astype(jnp.bfloat16).reshape(per * fr, keys.shape[0])
        mixed = jnp.dot(weights, values, preferred_element_type=jnp.float32)
        out = mixed[:fr]
        for h in range(1, per):
            out = jnp.where(lane == h, mixed[h * fr : (h + 1) * fr], out)
        return out.astype(jnp.bfloat16)

    def causal(b):
        span = pl.ds(pl.multiple_of(b * fr, fr), lead + fr)
        shape = (fr, lead + fr)
        row = lax.broadcasted_iota(jnp.int32, shape, 0)
        col = lax.broadcasted_iota(jnp.int32, shape, 1)
        spos = (b - LEFT_MAX) * fr + col
        tpos = b * fr + row
        apart = LEFT_MAX - col // fr
        allowed = (spos >= 0) & (spos <= tpos) & (apart <= count)
        allowed = allowed & ((spos < length) | (spos == tpos))
        return attend_block(q1[at_rows(b, fr), :], k1[span, :], v1[span, :], allowed)

    def ahead(b):
        span = pl.ds(pl.multiple_of(b * fr, fr), 2 * fr)
        shape = (fr, 2 * fr)
        row = lax.broadcasted_iota(jnp.int32, shape, 0)
        col = lax.broadcasted_iota(jnp.int32, shape, 1)
        spos = b * fr + col
        allowed = (col <= row + RIGHT) & ((spos < length) | (col == row))
        out = attend_block(q2[at_rows(b, fr), :], k2[span, :], v2[span, :], allowed)
        valid = b * fr + lax.broadcasted_iota(jnp.int32, (fr, cols), 0) < length
        return jnp.where(valid, out, jnp.zeros_like(out))

    def back_copy(which, d):
        src, dst = ((ctx1s, ctx1), (ctx2s, ctx2))[which]
        b = lax.rem(t + d, n)
        return pltpu.make_async_remote_copy(
            src_ref=src.at[at_rows(b, fr), :],
            dst_ref=dst.at[:, pl.ds(mine, cols)],
            send_sem=a2_send.at[which, d], recv_sem=a2_recv.at[which, d],
            device_id=(b, z), device_id_type=MESH,
        )

    def back_wait(which):
        src, dst = ((ctx1s, ctx1), (ctx2s, ctx2))[which]
        for d in range(1, n):
            b = lax.rem(t + n - d, n)
            pltpu.make_async_remote_copy(
                src_ref=src.at[at_rows(b, fr), :],
                dst_ref=dst.at[:, at_cols(b)],
                send_sem=a2_send.at[which, d], recv_sem=a2_recv.at[which, d],
                device_id=(b, z), device_id_type=MESH,
            ).wait_recv()

    def blocks(which, first, last):
        fun, src = ((causal, ctx1s), (ahead, ctx2s))[which]

        def body(d, carry):
            b = lax.rem(t + d, n)
            src[at_rows(b, fr), :] = fun(b)
            back_copy(which, d).start()
            return carry

        lax.fori_loop(first, last, body, 0)

    def own_block(which):
        fun, src, dst = ((causal, ctx1s, ctx1), (ahead, ctx2s, ctx2))[which]
        out = fun(t)
        src[at_rows(t, fr), :] = out
        dst[:, pl.ds(mine, cols)] = out

    ag_start(2)
    blocks(0, 1, n // 2)
    ag_forward(1)
    for step in range(1, nz - 1):
        chain(2, step)
    blocks(0, n // 2, n)
    own_block(0)
    ag_forward(2)
    back_wait(0)
    ag_wait(2, 0)
    for j in range(1, chips):
        ag_wait(2, chips + j - 1)

    mixed = jnp.dot(ctx1[...], wo[...], preferred_element_type=jnp.float32)
    hidden = (frames_ref[...].astype(jnp.float32) + mixed).astype(jnp.bfloat16)
    nbuf2[t] = norm_rows(hidden, gain_two_ref[...])
    ag_start(3)
    chain_end(2)
    ag_wait(3, 0)
    project(nbuf2, w2, q2, k2, v2, 0, t // 2)
    ag_forward(3)
    for j in range(1, chips):
        ag_wait(3, chips + j - 1)
        project(nbuf2, w2, q2, k2, v2, 0, flip(t, 2 * j) // 2)
    blocks(1, 1, n)
    own_block(1)

    ag_wait(1, 0)
    for j in range(1, chips):
        ag_wait(1, chips + j - 1)

    def term(zz):
        return jnp.dot(
            cott[at_rows(zz, rows), :], ctx2s[...], preferred_element_type=jnp.float32
        )

    def z_copy(d, back):
        to = lax.rem(z + d, nz)
        return pltpu.make_async_remote_copy(
            src_ref=gsend.at[d], dst_ref=grecv.at[d],
            send_sem=z_send.at[d], recv_sem=z_recv.at[d],
            device_id=(t, to), device_id_type=MESH,
        )

    for d in range(1, nz):
        gsend[d] = term(lax.rem(z + d, nz)).astype(jnp.bfloat16)
        z_copy(d, False).start()
    total = term(z)
    for d in range(1, nz):
        z_copy(d, True).wait_recv()
        total = total + grecv[d].astype(jnp.float32)
    gsum[...] = total

    def g_copy(d):
        b = lax.rem(t + d, n)
        return pltpu.make_async_remote_copy(
            src_ref=gsum.at[at_rows(b, part), :],
            dst_ref=wgr.at[:, pl.ds(mine, cols)],
            send_sem=a2_send.at[2, d], recv_sem=a2_recv.at[2, d],
            device_id=(b, z), device_id_type=MESH,
        )

    for d in range(1, n):
        g_copy(d).start()
    wgr[:, pl.ds(mine, cols)] = gsum[at_rows(t, part), :]
    back_wait(1)
    context_ref[...] = ctx2[...]
    for d in range(1, n):
        b = lax.rem(t + n - d, n)
        pltpu.make_async_remote_copy(
            src_ref=gsum.at[at_rows(b, part), :],
            dst_ref=wgr.at[:, at_cols(b)],
            send_sem=a2_send.at[2, d], recv_sem=a2_recv.at[2, d],
            device_id=(b, z), device_id_type=MESH,
        ).wait_recv()
    grad_ref[...] = wgr[...]
    for which in range(4):
        ag_sent(which)
    for which in range(3):
        chain_sent(which)
    for d in range(1, n):
        back_copy(0, d).wait_send()
        back_copy(1, d).wait_send()
        g_copy(d).wait_send()
    for d in range(1, nz):
        z_copy(d, False).wait_send()


def by_heads(
    n, nz, frames, gain_one, qkv_one, out_one, gain_two, qkv_two, lengths, left_counts, cotangent
):
    _, fr, width = frames.shape
    cols = width // n
    rows = width // nz
    span = n * fr
    vmem = pl.BlockSpec(memory_space=pltpu.VMEM)
    smem = pl.BlockSpec(memory_space=pltpu.SMEM)
    hbm = pl.BlockSpec(memory_space=pl.ANY)
    bf16, f32 = jnp.bfloat16, jnp.float32
    dma = pltpu.SemaphoreType.DMA
    context, grad = pl.pallas_call(
        functools.partial(heads_kernel, n, nz),
        out_shape=(
            jax.ShapeDtypeStruct((fr, width), bf16),
            jax.ShapeDtypeStruct((rows // n, width), f32),
        ),
        in_specs=[vmem, vmem, hbm, hbm, vmem, hbm, smem, smem, hbm],
        out_specs=(vmem, vmem),
        scratch_shapes=[
            pltpu.VMEM((n, fr, width), bf16),
            pltpu.VMEM((n, fr, width), bf16),
            pltpu.VMEM((width, 3 * cols), bf16),
            pltpu.VMEM((width, 3 * cols), bf16),
            pltpu.VMEM((width, width), bf16),
            pltpu.VMEM((fr, width), bf16),
            pltpu.VMEM((width, span), bf16),
            pltpu.VMEM((span, cols), bf16),
            pltpu.VMEM((span + LEFT_MAX * fr, cols), bf16),
            pltpu.VMEM((span + LEFT_MAX * fr, cols), bf16),
            pltpu.VMEM((span, cols), bf16),
            pltpu.VMEM((fr, width), bf16),
            pltpu.VMEM((span, cols), bf16),
            pltpu.VMEM((span + fr, cols), bf16),
            pltpu.VMEM((span + fr, cols), bf16),
            pltpu.VMEM((span, cols), bf16),
            pltpu.VMEM((fr, width), bf16),
            pltpu.VMEM((nz, rows, cols), bf16),
            pltpu.VMEM((nz, rows, cols), bf16),
            pltpu.VMEM((rows, cols), f32),
            pltpu.VMEM((rows // n, width), f32),
            dma((8,)),
            dma((4, n - 1)),
            dma((4, n - 1)),
            dma((3, 2, nz, 2)),
            dma((3, nz, 2)),
            dma((3, n)),
            dma((3, n)),
            dma((nz,)),
            dma((nz,)),
        ],
        compiler_params=pltpu.CompilerParams(
            collective_id=0, has_side_effects=True, vmem_limit_bytes=60 * 1024 * 1024
        ),
    )(
        frames[0], gain_one[None], qkv_one, out_one, gain_two[None], qkv_two,
        lengths, left_counts, cotangent[0],
    )
    return (context[None], grad)


def solution(mesh):
    n_tm = mesh.shape["tm"]
    even = n_tm > 2 and n_tm & (n_tm - 1) == 0 and HEADS % n_tm == 0
    chosen = functools.partial(by_heads, n_tm, mesh.shape["fsdp"]) if even else on_device
    in_specs = (
        P("fsdp", "tm", None),
        P(),
        P("fsdp", None),
        P("fsdp", None),
        P(),
        P("fsdp", None),
        P("fsdp"),
        P("fsdp"),
        P("fsdp", "tm", None),
    )
    out_specs = (P("fsdp", "tm", None), P(("tm", "fsdp"), None))
    return jax.shard_map(
        chosen, mesh=mesh, in_specs=in_specs, out_specs=out_specs, check_vma=False
    )
```

```python
import functools

import jax
import jax.numpy as jnp
from jax import lax
from jax.experimental import pallas as pl
from jax.experimental.pallas import tpu as pltpu
from jax.sharding import PartitionSpec as P

HEADS = 16
LEFT_MAX = 2
RIGHT = 23
CHIPS = 4


def from_behind(block, axis, distance):
    devices = range(lax.axis_size(axis))
    route = [(i - distance, i) for i in devices if i - distance in devices]
    return lax.ppermute(block, axis, route)


def norm_rows(values, gain):
    wide = values.astype(jnp.float32)
    mean = jnp.mean(wide, axis=-1, keepdims=True)
    var = jnp.mean((wide - mean) ** 2, axis=-1, keepdims=True)
    return ((wide - mean) * lax.rsqrt(var + 1e-05) * gain).astype(jnp.bfloat16)


def attend(query, keys, values, allowed, heads):
    rows_q, width = query.shape
    head = width // heads
    scale = 1.0 / head**0.5
    q_heads = query.reshape(rows_q, heads, head)
    k_heads = keys.reshape(keys.shape[0], heads, head)
    v_heads = values.reshape(values.shape[0], heads, head)
    scores = (
        jnp.einsum("qhe,khe->hqk", q_heads, k_heads, preferred_element_type=jnp.float32) * scale
    )
    scores = jnp.where(allowed[None], scores, -1e30)
    top = jnp.max(scores, axis=-1, keepdims=True)
    expo = jnp.exp(scores - top)
    weights = (expo / jnp.sum(expo, axis=-1, keepdims=True)).astype(jnp.bfloat16)
    ctx = jnp.einsum("hqk,khe->qhe", weights, v_heads, preferred_element_type=jnp.float32)
    return ctx.reshape(rows_q, width).astype(jnp.bfloat16)


def add_rows(left, piece):
    return jnp.dot(left, piece, preferred_element_type=jnp.float32)


def on_device(
    frames, gain_one, qkv_one, out_one, gain_two, qkv_two, lengths, left_counts, cotangent
):
    local = frames[0]
    grad_in = cotangent[0]
    fr, width = local.shape
    block = lax.axis_index("tm")
    length = lengths[0]
    count = left_counts[0]
    norm_one = norm_rows(local, gain_one)
    proj = add_rows(norm_one, lax.all_gather(qkv_one, "fsdp", axis=0, tiled=True))
    proj = proj.astype(jnp.bfloat16)
    query = proj[:, :width]
    key_value = proj[:, width:]
    earlier = [from_behind(key_value, "tm", step) for step in range(LEFT_MAX, 0, -1)]
    gathered = jnp.concatenate(earlier + [key_value], axis=0)
    rows = jnp.arange(fr, dtype=jnp.int32)
    cols = jnp.arange((LEFT_MAX + 1) * fr, dtype=jnp.int32)
    tpos = block * fr + rows[:, None]
    spos = (block - LEFT_MAX) * fr + cols[None, :]
    apart = LEFT_MAX - cols[None, :] // fr
    allowed = (spos >= 0) & (spos <= tpos) & (apart <= count) & ((spos < length) | (spos == tpos))
    ctx_one = attend(query, gathered[:, :width], gathered[:, width:], allowed, HEADS)
    out_proj = add_rows(ctx_one, lax.all_gather(out_one, "fsdp", axis=0, tiled=True))
    hidden = (local.astype(jnp.float32) + out_proj).astype(jnp.bfloat16)
    norm_two = norm_rows(hidden, gain_two)
    proj2 = add_rows(norm_two, lax.all_gather(qkv_two, "fsdp", axis=0, tiled=True))
    proj2 = proj2.astype(jnp.bfloat16)
    query2 = proj2[:, :width]
    key_value2 = proj2[:, width:]
    ahead = from_behind(key_value2[:RIGHT], "tm", -1)
    joined = jnp.concatenate([key_value2, ahead], axis=0)
    cols2 = jnp.arange(fr + RIGHT, dtype=jnp.int32)
    spos2 = block * fr + cols2[None, :]
    allowed2 = (cols2[None, :] <= rows[:, None] + RIGHT) & ((spos2 < length) | (spos2 == tpos))
    ctx_two = attend(query2, joined[:, :width], joined[:, width:], allowed2, HEADS)
    valid = block * fr + rows < length
    context = jnp.where(valid[:, None], ctx_two, jnp.zeros_like(ctx_two))
    weight_grad = lax.psum_scatter(
        lax.dot_general(
            grad_in, context, (((0,), (0,)), ((), ())), preferred_element_type=jnp.float32
        ),
        ("tm", "fsdp"),
        scatter_dimension=0,
        tiled=True,
    )
    return (context[None], weight_grad)


MESH = pl.DeviceIdType.MESH


def flip(index, mask):
    out, bit = index, 1
    while bit <= mask:
        if mask & bit:
            out = out + bit * (1 - 2 * ((index // bit) % 2))
        bit *= 2
    return out


def heads_kernel(
    n,
    nz,
    frames_ref, gain_one_ref, qkv_one_ref, out_one_ref, gain_two_ref, qkv_two_ref,
    length_ref, count_ref, cot_ref,
    context_ref, grad_ref,
    nbuf, nbuf2, w1, w2, wo, cotv, cott, q1, k1, v1, ctx1s, ctx1, q2, k2, v2, ctx2s, ctx2,
    gsend, grecv, gsum, wgr,
    local_sem, ag_send, ag_recv, ch_send, ch_recv, a2_send, a2_recv, z_send, z_recv,
):
    t = lax.axis_index("tm")
    z = lax.axis_index("fsdp")
    fr, width = frames_ref.shape
    cols = width // n
    head = width // HEADS
    per = HEADS // n
    rows = width // nz
    part = rows // n
    scale = 1.0 / head**0.5
    mine = pl.multiple_of(t * cols, cols)

    def at_cols(index):
        return pl.ds(pl.multiple_of(index * cols, cols), cols)

    def at_rows(index, size):
        return pl.ds(pl.multiple_of(index * size, size), size)

    own_rows = at_rows(z, rows)
    local = []
    for j in range(3):
        for which, (src, dst) in enumerate(((qkv_one_ref, w1), (qkv_two_ref, w2))):
            local.append(
                pltpu.make_async_copy(
                    src.at[:, pl.ds(pl.multiple_of(j * width + mine, cols), cols)],
                    dst.at[own_rows, pl.ds(j * cols, cols)],
                    local_sem.at[2 * j + which],
                )
            )
    local.append(
        pltpu.make_async_copy(
            out_one_ref.at[:, pl.ds(mine, cols)], wo.at[own_rows, pl.ds(mine, cols)], local_sem.at[6]
        )
    )
    local.append(pltpu.make_async_copy(cot_ref, cotv, local_sem.at[7]))
    for copy in (local[6], local[0], local[2], local[4], local[7], local[1], local[3], local[5]):
        copy.start()

    barrier = pltpu.get_barrier_semaphore()
    for d in range(1, n):
        pl.semaphore_signal(
            barrier, inc=1, device_id=(lax.rem(t + d, n), z), device_id_type=MESH
        )
    for d in range(1, nz):
        pl.semaphore_signal(
            barrier, inc=1, device_id=(t, lax.rem(z + d, nz)), device_id_type=MESH
        )
    pl.semaphore_wait(barrier, n + nz - 2)

    half = rows // 2

    def chain_view(which, shard, h):
        span = pl.ds(pl.multiple_of(shard * rows + h * half, half), half)
        if which == 1:
            return wo.at[span, pl.ds(mine, cols)]
        return (w1, None, w2)[which].at[span, :]

    def chain_copy(which, step, up, h):
        shard = z - step if up else z + step
        shard = jnp.clip(shard, 0, nz - 1)
        to = jnp.clip(z + 1 if up else z - 1, 0, nz - 1)
        view = chain_view(which, shard, h)
        return pltpu.make_async_remote_copy(
            src_ref=view,
            dst_ref=view,
            send_sem=ch_send.at[which, 0 if up else 1, step, h],
            recv_sem=ch_recv.at[which, shard, h],
            device_id=(t, to),
            device_id_type=MESH,
        )

    def chain_cond(step, up):
        if up:
            return (z >= step) & (z < nz - 1)
        return (z + step < nz) & (z > 0)

    def chain(which, step):
        for h in range(2):
            for up in (True, False):
                @pl.when(chain_cond(step, up))
                def _():
                    copy = chain_copy(which, step, up, h)
                    if step:
                        copy.wait_recv()
                    copy.start()

    def chain_end(which):
        for edge, up in ((nz - 1, True), (0, False)):
            @pl.when(z == edge)
            def _():
                for step in range(1, nz):
                    for h in range(2):
                        shard = edge - step if up else edge + step
                        view = chain_view(which, shard, h)
                        pltpu.make_async_remote_copy(
                            src_ref=view,
                            dst_ref=view,
                            send_sem=ch_send.at[which, 0, 0, h],
                            recv_sem=ch_recv.at[which, shard, h],
                            device_id=(t, edge - 1 if up else edge + 1),
                            device_id_type=MESH,
                        ).wait_recv()

    def chain_sent(which):
        for step in range(nz - 1):
            for up in (True, False):
                for h in range(2):
                    @pl.when(chain_cond(step, up))
                    def _():
                        chain_copy(which, step, up, h).wait_send()

    def ag_view(which, index, piece):
        if which in (0, 3):
            buf = (nbuf, None, None, nbuf2)[which]
            if piece is None:
                return buf.at[index]
            return buf.at[index, pl.ds(piece * (fr // 2), fr // 2), :]
        buf = (None, cott, wo)[which]
        if piece is None:
            return buf.at[:, at_cols(index)]
        return buf.at[pl.ds(piece * (width // 2), width // 2), at_cols(index)]

    slots = (
        (0, None, 1), (0, 0, 2), (0, 1, 2), (0, 1, 4), (0, 0, 4),
        (2, 0, 4), (4, 1, 2),
        (2, None, 1), (4, None, 1), (6, 0, 1), (6, 1, 1),
    )

    def ag_copy(which, slot):
        block, piece, to = slots[slot]
        view = ag_view(which, flip(t, block), piece)
        return pltpu.make_async_remote_copy(
            src_ref=view, dst_ref=view,
            send_sem=ag_send.at[which, slot], recv_sem=ag_recv.at[which, slot],
            device_id=(flip(t, to), z), device_id_type=MESH,
        )

    def ag_wait(which, slot):
        block, piece, to = slots[slot]
        view = ag_view(which, flip(t, block ^ to), piece)
        pltpu.make_async_remote_copy(
            src_ref=view, dst_ref=view,
            send_sem=ag_send.at[which, slot], recv_sem=ag_recv.at[which, slot],
            device_id=(flip(t, to), z), device_id_type=MESH,
        ).wait_recv()

    def ag_start(which):
        for slot in (1, 3, 2, 4, 0):
            ag_copy(which, slot).start()

    def ag_forward(which, stage):
        for waits, slot in (
            (((1, 5), (3, 6)), ((2, 7), (4, 8)), ((5, 9), (6, 10)))[stage]
        ):
            ag_wait(which, waits)
            ag_copy(which, slot).start()

    def ag_partner(which):
        for slot in (0, 7, 8, 9, 10):
            ag_wait(which, slot)

    def ag_sent(which):
        for slot in range(len(slots)):
            ag_copy(which, slot).wait_send()

    local[6].wait()
    chain(1, 0)
    for j in (0, 2, 4):
        local[j].wait()
    chain(0, 0)
    nbuf[t] = norm_rows(frames_ref[...], gain_one_ref[...])
    ag_start(0)
    local[7].wait()
    turned = cotv[...].T
    for zz in range(nz):
        for tt in range(n):
            cott[zz * rows + tt * part : zz * rows + (tt + 1) * part, pl.ds(mine, cols)] = turned[
                (tt * nz + zz) * part : (tt * nz + zz + 1) * part
            ]
    lead = LEFT_MAX * fr
    zeros = jnp.zeros((lead, cols), jnp.bfloat16)
    k1[0:lead, :] = zeros
    v1[0:lead, :] = zeros
    k2[n * fr :, :] = zeros[:fr]
    v2[n * fr :, :] = zeros[:fr]
    chain(1, 1)
    ag_forward(0, 0)
    for step in range(2, nz - 1):
        chain(1, step)
    chain_end(1)
    ag_forward(0, 1)
    chain(0, 1)
    ag_forward(0, 2)
    ag_start(2)
    for step in range(2, nz - 1):
        chain(0, step)
    for j in (1, 3, 5):
        local[j].wait()
    chain(2, 0)

    def project(buf, weight, q, k, v, before, pair):
        left = buf[pl.ds(pair * 2, 2)].reshape(2 * fr, width)
        out = jnp.dot(left, weight[...], preferred_element_type=jnp.float32).astype(jnp.bfloat16)
        span = at_rows(pair, 2 * fr)
        q[span, :] = out[:, :cols]
        after = pl.ds(pl.multiple_of(pair * 2 * fr + before, fr), 2 * fr)
        k[after, :] = out[:, cols : 2 * cols]
        v[after, :] = out[:, 2 * cols :]

    ag_forward(2, 0)
    ag_forward(2, 1)
    ag_partner(0)
    ag_forward(2, 2)
    ag_start(1)
    chain_end(0)
    for j in range(n // 2):
        project(nbuf, w1, q1, k1, v1, lead, j)

    length = length_ref[0]
    count = count_ref[0]

    def attend_block(query, keys, values, allowed):
        lane = lax.broadcasted_iota(jnp.int32, (fr, cols), 1) // head
        blank = jnp.zeros_like(query)
        stacked = jnp.concatenate([jnp.where(lane == h, query, blank) for h in range(per)], axis=0)
        scores = lax.dot_general(
            stacked, keys, (((1,), (1,)), ((), ())), preferred_element_type=jnp.float32
        ) * scale
        scores = scores.reshape(per, fr, keys.shape[0])
        scores = jnp.where(allowed[None], scores, -1e30)
        top = jnp.max(scores, axis=-1, keepdims=True)
        expo = jnp.exp(scores - top)
        weights = expo * (1.0 / jnp.sum(expo, axis=-1, keepdims=True))
        weights = weights.astype(jnp.bfloat16).reshape(per * fr, keys.shape[0])
        mixed = jnp.dot(weights, values, preferred_element_type=jnp.float32)
        out = mixed[:fr]
        for h in range(1, per):
            out = jnp.where(lane == h, mixed[h * fr : (h + 1) * fr], out)
        return out.astype(jnp.bfloat16)

    def causal(b):
        span = pl.ds(pl.multiple_of(b * fr, fr), lead + fr)
        shape = (fr, lead + fr)
        row = lax.broadcasted_iota(jnp.int32, shape, 0)
        col = lax.broadcasted_iota(jnp.int32, shape, 1)
        spos = (b - LEFT_MAX) * fr + col
        tpos = b * fr + row
        apart = LEFT_MAX - col // fr
        allowed = (spos >= 0) & (spos <= tpos) & (apart <= count)
        allowed = allowed & ((spos < length) | (spos == tpos))
        return attend_block(q1[at_rows(b, fr), :], k1[span, :], v1[span, :], allowed)

    def ahead(b):
        span = pl.ds(pl.multiple_of(b * fr, fr), 2 * fr)
        shape = (fr, 2 * fr)
        row = lax.broadcasted_iota(jnp.int32, shape, 0)
        col = lax.broadcasted_iota(jnp.int32, shape, 1)
        spos = b * fr + col
        allowed = (col <= row + RIGHT) & ((spos < length) | (col == row))
        out = attend_block(q2[at_rows(b, fr), :], k2[span, :], v2[span, :], allowed)
        valid = b * fr + lax.broadcasted_iota(jnp.int32, (fr, cols), 0) < length
        return jnp.where(valid, out, jnp.zeros_like(out))

    def back_copy(which, d):
        src, dst = ((ctx1s, ctx1), (ctx2s, ctx2))[which]
        b = lax.rem(t + d, n)
        return pltpu.make_async_remote_copy(
            src_ref=src.at[at_rows(b, fr), :],
            dst_ref=dst.at[:, pl.ds(mine, cols)],
            send_sem=a2_send.at[which, d], recv_sem=a2_recv.at[which, d],
            device_id=(b, z), device_id_type=MESH,
        )

    def back_wait(which):
        src, dst = ((ctx1s, ctx1), (ctx2s, ctx2))[which]
        for d in range(1, n):
            b = lax.rem(t + n - d, n)
            pltpu.make_async_remote_copy(
                src_ref=src.at[at_rows(b, fr), :],
                dst_ref=dst.at[:, at_cols(b)],
                send_sem=a2_send.at[which, d], recv_sem=a2_recv.at[which, d],
                device_id=(b, z), device_id_type=MESH,
            ).wait_recv()

    def blocks(which, first, last):
        fun, src = ((causal, ctx1s), (ahead, ctx2s))[which]

        def body(d, carry):
            b = lax.rem(t + d, n)
            src[at_rows(b, fr), :] = fun(b)
            back_copy(which, d).start()
            return carry

        lax.fori_loop(first, last, body, 0)

    def own_block(which):
        fun, src, dst = ((causal, ctx1s, ctx1), (ahead, ctx2s, ctx2))[which]
        out = fun(t)
        src[at_rows(t, fr), :] = out
        dst[:, pl.ds(mine, cols)] = out

    blocks(0, 1, n // 2)
    ag_forward(1, 0)
    chain(2, 1)
    blocks(0, n // 2, n)
    own_block(0)
    ag_forward(1, 1)
    ag_partner(2)
    back_wait(0)

    mixed = jnp.dot(ctx1[...], wo[...], preferred_element_type=jnp.float32)
    hidden = (frames_ref[...].astype(jnp.float32) + mixed).astype(jnp.bfloat16)
    nbuf2[t] = norm_rows(hidden, gain_two_ref[...])
    ag_start(3)
    ag_forward(1, 2)
    for step in range(2, nz - 1):
        chain(2, step)
    ag_forward(3, 0)
    chain_end(2)
    ag_wait(3, 0)
    project(nbuf2, w2, q2, k2, v2, 0, t // 2)
    ag_forward(3, 1)
    ag_wait(3, 7)
    project(nbuf2, w2, q2, k2, v2, 0, flip(t, 2) // 2)
    ag_wait(3, 8)
    project(nbuf2, w2, q2, k2, v2, 0, flip(t, 4) // 2)
    ag_forward(3, 2)
    ag_wait(3, 9)
    ag_wait(3, 10)
    project(nbuf2, w2, q2, k2, v2, 0, flip(t, 6) // 2)
    blocks(1, 1, n)
    own_block(1)
    ag_partner(1)

    def term(zz):
        return jnp.dot(
            cott[at_rows(zz, rows), :], ctx2s[...], preferred_element_type=jnp.float32
        )

    def z_copy(d, back):
        to = lax.rem(z + d, nz)
        return pltpu.make_async_remote_copy(
            src_ref=gsend.at[d], dst_ref=grecv.at[d],
            send_sem=z_send.at[d], recv_sem=z_recv.at[d],
            device_id=(t, to), device_id_type=MESH,
        )

    for d in range(1, nz):
        gsend[d] = term(lax.rem(z + d, nz)).astype(jnp.bfloat16)
        z_copy(d, False).start()
    total = term(z)
    for d in range(1, nz):
        z_copy(d, True).wait_recv()
        total = total + grecv[d].astype(jnp.float32)
    gsum[...] = total

    def g_copy(d):
        b = lax.rem(t + d, n)
        return pltpu.make_async_remote_copy(
            src_ref=gsum.at[at_rows(b, part), :],
            dst_ref=wgr.at[:, pl.ds(mine, cols)],
            send_sem=a2_send.at[2, d], recv_sem=a2_recv.at[2, d],
            device_id=(b, z), device_id_type=MESH,
        )

    for d in range(1, n):
        g_copy(d).start()
    wgr[:, pl.ds(mine, cols)] = gsum[at_rows(t, part), :]
    back_wait(1)
    context_ref[...] = ctx2[...]
    for d in range(1, n):
        b = lax.rem(t + n - d, n)
        pltpu.make_async_remote_copy(
            src_ref=gsum.at[at_rows(b, part), :],
            dst_ref=wgr.at[:, at_cols(b)],
            send_sem=a2_send.at[2, d], recv_sem=a2_recv.at[2, d],
            device_id=(b, z), device_id_type=MESH,
        ).wait_recv()
    grad_ref[...] = wgr[...]
    for which in range(4):
        ag_sent(which)
    for which in range(3):
        chain_sent(which)
    for d in range(1, n):
        back_copy(0, d).wait_send()
        back_copy(1, d).wait_send()
        g_copy(d).wait_send()
    for d in range(1, nz):
        z_copy(d, False).wait_send()


def hand_out(context_ref, grad_ref, context_out, grad_out):
    context_out[...] = context_ref[...]
    grad_out[...] = grad_ref[...]


def by_heads(
    n, nz, frames, gain_one, qkv_one, out_one, gain_two, qkv_two, lengths, left_counts, cotangent
):
    _, fr, width = frames.shape
    cols = width // n
    rows = width // nz
    span = n * fr
    vmem = pl.BlockSpec(memory_space=pltpu.VMEM)
    smem = pl.BlockSpec(memory_space=pltpu.SMEM)
    hbm = pl.BlockSpec(memory_space=pl.ANY)
    bf16, f32 = jnp.bfloat16, jnp.float32
    dma = pltpu.SemaphoreType.DMA
    context, grad = pl.pallas_call(
        functools.partial(heads_kernel, n, nz),
        out_shape=(
            jax.ShapeDtypeStruct((fr, width), bf16),
            jax.ShapeDtypeStruct((rows // n, width), f32),
        ),
        in_specs=[vmem, vmem, hbm, hbm, vmem, hbm, smem, smem, hbm],
        out_specs=(vmem, vmem),
        scratch_shapes=[
            pltpu.VMEM((n, fr, width), bf16),
            pltpu.VMEM((n, fr, width), bf16),
            pltpu.VMEM((width, 3 * cols), bf16),
            pltpu.VMEM((width, 3 * cols), bf16),
            pltpu.VMEM((width, width), bf16),
            pltpu.VMEM((fr, width), bf16),
            pltpu.VMEM((width, span), bf16),
            pltpu.VMEM((span, cols), bf16),
            pltpu.VMEM((span + LEFT_MAX * fr, cols), bf16),
            pltpu.VMEM((span + LEFT_MAX * fr, cols), bf16),
            pltpu.VMEM((span, cols), bf16),
            pltpu.VMEM((fr, width), bf16),
            pltpu.VMEM((span, cols), bf16),
            pltpu.VMEM((span + fr, cols), bf16),
            pltpu.VMEM((span + fr, cols), bf16),
            pltpu.VMEM((span, cols), bf16),
            pltpu.VMEM((fr, width), bf16),
            pltpu.VMEM((nz, rows, cols), bf16),
            pltpu.VMEM((nz, rows, cols), bf16),
            pltpu.VMEM((rows, cols), f32),
            pltpu.VMEM((rows // n, width), f32),
            dma((8,)),
            dma((4, 11)),
            dma((4, 11)),
            dma((3, 2, nz, 2)),
            dma((3, nz, 2)),
            dma((3, n)),
            dma((3, n)),
            dma((nz,)),
            dma((nz,)),
        ],
        compiler_params=pltpu.CompilerParams(
            collective_id=0, has_side_effects=True, vmem_limit_bytes=60 * 1024 * 1024
        ),
    )(
        frames[0], gain_one[None], qkv_one, out_one, gain_two[None], qkv_two,
        lengths, left_counts, cotangent[0],
    )
    context, grad = pl.pallas_call(
        hand_out,
        out_shape=(
            jax.ShapeDtypeStruct((fr, width), bf16),
            jax.ShapeDtypeStruct((rows // n, width), f32),
        ),
        in_specs=[vmem, vmem],
        out_specs=(vmem, vmem),
    )(context, grad)
    return (context[None], grad)


def solution(mesh):
    n_tm = mesh.shape["tm"]
    even = n_tm == 2 * CHIPS and HEADS % n_tm == 0
    chosen = functools.partial(by_heads, n_tm, mesh.shape["fsdp"]) if even else on_device
    in_specs = (
        P("fsdp", "tm", None),
        P(),
        P("fsdp", None),
        P("fsdp", None),
        P(),
        P("fsdp", None),
        P("fsdp"),
        P("fsdp"),
        P("fsdp", "tm", None),
    )
    out_specs = (P("fsdp", "tm", None), P(("tm", "fsdp"), None))
    return jax.shard_map(
        chosen, mesh=mesh, in_specs=in_specs, out_specs=out_specs, check_vma=False
    )
```

```python
import functools

import jax
import jax.numpy as jnp
from jax import lax
from jax.experimental import pallas as pl
from jax.experimental.pallas import tpu as pltpu
from jax.sharding import PartitionSpec as P

HEADS = 16
LEFT_MAX = 2
RIGHT = 23
CHIPS = 4


def from_behind(block, axis, distance):
    devices = range(lax.axis_size(axis))
    route = [(i - distance, i) for i in devices if i - distance in devices]
    return lax.ppermute(block, axis, route)


def norm_rows(values, gain):
    wide = values.astype(jnp.float32)
    mean = jnp.mean(wide, axis=-1, keepdims=True)
    var = jnp.mean((wide - mean) ** 2, axis=-1, keepdims=True)
    return ((wide - mean) * lax.rsqrt(var + 1e-05) * gain).astype(jnp.bfloat16)


def attend(query, keys, values, allowed, heads):
    rows_q, width = query.shape
    head = width // heads
    scale = 1.0 / head**0.5
    q_heads = query.reshape(rows_q, heads, head)
    k_heads = keys.reshape(keys.shape[0], heads, head)
    v_heads = values.reshape(values.shape[0], heads, head)
    scores = (
        jnp.einsum("qhe,khe->hqk", q_heads, k_heads, preferred_element_type=jnp.float32) * scale
    )
    scores = jnp.where(allowed[None], scores, -1e30)
    top = jnp.max(scores, axis=-1, keepdims=True)
    expo = jnp.exp(scores - top)
    weights = (expo / jnp.sum(expo, axis=-1, keepdims=True)).astype(jnp.bfloat16)
    ctx = jnp.einsum("hqk,khe->qhe", weights, v_heads, preferred_element_type=jnp.float32)
    return ctx.reshape(rows_q, width).astype(jnp.bfloat16)


def add_rows(left, piece):
    return jnp.dot(left, piece, preferred_element_type=jnp.float32)


def on_device(
    frames, gain_one, qkv_one, out_one, gain_two, qkv_two, lengths, left_counts, cotangent
):
    local = frames[0]
    grad_in = cotangent[0]
    fr, width = local.shape
    block = lax.axis_index("tm")
    length = lengths[0]
    count = left_counts[0]
    norm_one = norm_rows(local, gain_one)
    proj = add_rows(norm_one, lax.all_gather(qkv_one, "fsdp", axis=0, tiled=True))
    proj = proj.astype(jnp.bfloat16)
    query = proj[:, :width]
    key_value = proj[:, width:]
    earlier = [from_behind(key_value, "tm", step) for step in range(LEFT_MAX, 0, -1)]
    gathered = jnp.concatenate(earlier + [key_value], axis=0)
    rows = jnp.arange(fr, dtype=jnp.int32)
    cols = jnp.arange((LEFT_MAX + 1) * fr, dtype=jnp.int32)
    tpos = block * fr + rows[:, None]
    spos = (block - LEFT_MAX) * fr + cols[None, :]
    apart = LEFT_MAX - cols[None, :] // fr
    allowed = (spos >= 0) & (spos <= tpos) & (apart <= count) & ((spos < length) | (spos == tpos))
    ctx_one = attend(query, gathered[:, :width], gathered[:, width:], allowed, HEADS)
    out_proj = add_rows(ctx_one, lax.all_gather(out_one, "fsdp", axis=0, tiled=True))
    hidden = (local.astype(jnp.float32) + out_proj).astype(jnp.bfloat16)
    norm_two = norm_rows(hidden, gain_two)
    proj2 = add_rows(norm_two, lax.all_gather(qkv_two, "fsdp", axis=0, tiled=True))
    proj2 = proj2.astype(jnp.bfloat16)
    query2 = proj2[:, :width]
    key_value2 = proj2[:, width:]
    ahead = from_behind(key_value2[:RIGHT], "tm", -1)
    joined = jnp.concatenate([key_value2, ahead], axis=0)
    cols2 = jnp.arange(fr + RIGHT, dtype=jnp.int32)
    spos2 = block * fr + cols2[None, :]
    allowed2 = (cols2[None, :] <= rows[:, None] + RIGHT) & ((spos2 < length) | (spos2 == tpos))
    ctx_two = attend(query2, joined[:, :width], joined[:, width:], allowed2, HEADS)
    valid = block * fr + rows < length
    context = jnp.where(valid[:, None], ctx_two, jnp.zeros_like(ctx_two))
    weight_grad = lax.psum_scatter(
        lax.dot_general(
            grad_in, context, (((0,), (0,)), ((), ())), preferred_element_type=jnp.float32
        ),
        ("tm", "fsdp"),
        scatter_dimension=0,
        tiled=True,
    )
    return (context[None], weight_grad)


MESH = pl.DeviceIdType.MESH


def flip(index, mask):
    out, bit = index, 1
    while bit <= mask:
        if mask & bit:
            out = out + bit * (1 - 2 * ((index // bit) % 2))
        bit *= 2
    return out


def heads_kernel(
    n,
    nz,
    frames_ref, gain_one_ref, qkv_one_ref, out_one_ref, gain_two_ref, qkv_two_ref,
    length_ref, count_ref, cot_ref,
    context_ref, grad_ref,
    nbuf, nbuf2, w1, w2, wo, cotv, cott, q1, k1, v1, ctx1s, ctx1, q2, k2, v2, ctx2s, ctx2,
    gsend, grecv, gsum, wgr,
    local_sem, ag_send, ag_recv, ch_send, ch_recv, a2_send, a2_recv, z_send, z_recv,
):
    t = lax.axis_index("tm")
    z = lax.axis_index("fsdp")
    fr, width = frames_ref.shape
    cols = width // n
    head = width // HEADS
    per = HEADS // n
    rows = width // nz
    part = rows // n
    scale = 1.0 / head**0.5
    mine = pl.multiple_of(t * cols, cols)

    def at_cols(index):
        return pl.ds(pl.multiple_of(index * cols, cols), cols)

    def at_rows(index, size):
        return pl.ds(pl.multiple_of(index * size, size), size)

    own_rows = at_rows(z, rows)
    local = []
    for j in range(3):
        for which, (src, dst) in enumerate(((qkv_one_ref, w1), (qkv_two_ref, w2))):
            local.append(
                pltpu.make_async_copy(
                    src.at[:, pl.ds(pl.multiple_of(j * width + mine, cols), cols)],
                    dst.at[own_rows, pl.ds(j * cols, cols)],
                    local_sem.at[2 * j + which],
                )
            )
    local.append(
        pltpu.make_async_copy(
            out_one_ref, wo.at[pl.ds(0, rows), :], local_sem.at[6]
        )
    )
    local.append(pltpu.make_async_copy(cot_ref, cotv, local_sem.at[7]))
    for copy in (local[6], local[0], local[2], local[4], local[7], local[1], local[3], local[5]):
        copy.start()

    barrier = pltpu.get_barrier_semaphore()
    for d in range(1, n):
        pl.semaphore_signal(
            barrier, inc=1, device_id=(lax.rem(t + d, n), z), device_id_type=MESH
        )
    for d in range(1, nz):
        pl.semaphore_signal(
            barrier, inc=1, device_id=(t, lax.rem(z + d, nz)), device_id_type=MESH
        )
    pl.semaphore_wait(barrier, n + nz - 2)

    half = rows // 2

    def chain_view(which, shard, h, at):
        place = lax.rem(shard - at + nz, nz) if which == 1 else shard
        span = pl.ds(pl.multiple_of(place * rows + h * half, half), half)
        if which == 1:
            return wo.at[span, pl.ds(mine, cols)]
        return (w1, None, w2)[which].at[span, :]

    def chain_copy(which, step, up, h):
        shard = z - step if up else z + step
        shard = jnp.clip(shard, 0, nz - 1)
        to = jnp.clip(z + 1 if up else z - 1, 0, nz - 1)
        return pltpu.make_async_remote_copy(
            src_ref=chain_view(which, shard, h, z),
            dst_ref=chain_view(which, shard, h, to),
            send_sem=ch_send.at[which, 0 if up else 1, step, h],
            recv_sem=ch_recv.at[which, shard, h],
            device_id=(t, to),
            device_id_type=MESH,
        )

    def chain_wait(which, shard, h, other):
        view = chain_view(which, shard, h, z)
        pltpu.make_async_remote_copy(
            src_ref=view,
            dst_ref=view,
            send_sem=ch_send.at[which, 0, 0, h],
            recv_sem=ch_recv.at[which, shard, h],
            device_id=(t, other),
            device_id_type=MESH,
        ).wait_recv()

    def chain_cond(step, up):
        if up:
            return (z >= step) & (z < nz - 1)
        return (z + step < nz) & (z > 0)

    def chain(which, step):
        for h in range(2):
            for up in (True, False):
                @pl.when(chain_cond(step, up))
                def _():
                    copy = chain_copy(which, step, up, h)
                    if step:
                        chain_wait(which, z - step if up else z + step, h, z + 1 if up else z - 1)
                    copy.start()

    def chain_end(which):
        for edge, up in ((nz - 1, True), (0, False)):
            @pl.when(z == edge)
            def _():
                for step in range(1, nz):
                    for h in range(2):
                        shard = edge - step if up else edge + step
                        chain_wait(which, shard, h, edge - 1 if up else edge + 1)

    def chain_sent(which):
        for step in range(nz - 1):
            for up in (True, False):
                for h in range(2):
                    @pl.when(chain_cond(step, up))
                    def _():
                        chain_copy(which, step, up, h).wait_send()

    def ag_view(which, index, piece):
        if which in (0, 3):
            buf = (nbuf, None, None, nbuf2)[which]
            if piece is None:
                return buf.at[index]
            return buf.at[index, pl.ds(piece * (fr // 2), fr // 2), :]
        buf, first = ((None, 0), (cott, 0), (wo, rows))[which]
        size = width - first
        if piece is None:
            return buf.at[pl.ds(first, size), at_cols(index)]
        return buf.at[pl.ds(first + piece * (size // 2), size // 2), at_cols(index)]

    slots = (
        (0, None, 1), (0, 0, 2), (0, 1, 2), (0, 1, 4), (0, 0, 4),
        (2, 0, 4), (4, 1, 2),
        (2, None, 1), (4, None, 1), (6, 0, 1), (6, 1, 1),
    )

    def ag_copy(which, slot):
        block, piece, to = slots[slot]
        view = ag_view(which, flip(t, block), piece)
        return pltpu.make_async_remote_copy(
            src_ref=view, dst_ref=view,
            send_sem=ag_send.at[which, slot], recv_sem=ag_recv.at[which, slot],
            device_id=(flip(t, to), z), device_id_type=MESH,
        )

    def ag_wait(which, slot):
        block, piece, to = slots[slot]
        view = ag_view(which, flip(t, block ^ to), piece)
        pltpu.make_async_remote_copy(
            src_ref=view, dst_ref=view,
            send_sem=ag_send.at[which, slot], recv_sem=ag_recv.at[which, slot],
            device_id=(flip(t, to), z), device_id_type=MESH,
        ).wait_recv()

    def ag_start(which):
        for slot in (1, 3, 2, 4, 0):
            ag_copy(which, slot).start()

    def ag_forward(which, stage):
        for waits, slot in (
            (((1, 5), (3, 6)), ((2, 7), (4, 8)), ((5, 9), (6, 10)))[stage]
        ):
            ag_wait(which, waits)
            ag_copy(which, slot).start()

    def ag_partner(which):
        for slot in (0, 7, 8, 9, 10):
            ag_wait(which, slot)

    def ag_sent(which):
        for slot in range(len(slots)):
            ag_copy(which, slot).wait_send()

    for j in (0, 2, 4):
        local[j].wait()
    chain(0, 0)
    local[6].wait()
    nbuf[t] = norm_rows(frames_ref[...], gain_one_ref[...])
    ag_start(0)
    local[7].wait()
    turned = cotv[...].T
    for zz in range(nz):
        for tt in range(n):
            cott[zz * rows + tt * part : zz * rows + (tt + 1) * part, pl.ds(mine, cols)] = turned[
                (tt * nz + zz) * part : (tt * nz + zz + 1) * part
            ]
    lead = LEFT_MAX * fr
    zeros = jnp.zeros((lead, cols), jnp.bfloat16)
    k1[0:lead, :] = zeros
    v1[0:lead, :] = zeros
    k2[n * fr :, :] = zeros[:fr]
    v2[n * fr :, :] = zeros[:fr]
    ag_forward(0, 0)
    chain(0, 1)
    chain(1, 0)
    ag_forward(0, 1)
    chain(0, 2)
    ag_forward(0, 2)
    ag_start(1)
    chain(1, 1)
    chain(1, 2)
    for j in (1, 3, 5):
        local[j].wait()
    chain(2, 0)

    def project(buf, weight, q, k, v, before, pair):
        left = buf[pl.ds(pair * 2, 2)].reshape(2 * fr, width)
        out = jnp.dot(left, weight[...], preferred_element_type=jnp.float32).astype(jnp.bfloat16)
        span = at_rows(pair, 2 * fr)
        q[span, :] = out[:, :cols]
        after = pl.ds(pl.multiple_of(pair * 2 * fr + before, fr), 2 * fr)
        k[after, :] = out[:, cols : 2 * cols]
        v[after, :] = out[:, 2 * cols :]

    ag_partner(0)
    chain_end(0)
    ag_forward(1, 0)
    for j in range(n // 2):
        project(nbuf, w1, q1, k1, v1, lead, j)
    chain_end(1)
    ag_start(2)
    ag_forward(1, 1)

    length = length_ref[0]
    count = count_ref[0]

    def attend_block(query, keys, values, allowed):
        lane = lax.broadcasted_iota(jnp.int32, (fr, cols), 1) // head
        blank = jnp.zeros_like(query)
        stacked = jnp.concatenate([jnp.where(lane == h, query, blank) for h in range(per)], axis=0)
        scores = lax.dot_general(
            stacked, keys, (((1,), (1,)), ((), ())), preferred_element_type=jnp.float32
        ) * scale
        scores = scores.reshape(per, fr, keys.shape[0])
        scores = jnp.where(allowed[None], scores, -1e30)
        top = jnp.max(scores, axis=-1, keepdims=True)
        expo = jnp.exp(scores - top)
        weights = expo * (1.0 / jnp.sum(expo, axis=-1, keepdims=True))
        weights = weights.astype(jnp.bfloat16).reshape(per * fr, keys.shape[0])
        mixed = jnp.dot(weights, values, preferred_element_type=jnp.float32)
        out = mixed[:fr]
        for h in range(1, per):
            out = jnp.where(lane == h, mixed[h * fr : (h + 1) * fr], out)
        return out.astype(jnp.bfloat16)

    def causal(b):
        span = pl.ds(pl.multiple_of(b * fr, fr), lead + fr)
        shape = (fr, lead + fr)
        row = lax.broadcasted_iota(jnp.int32, shape, 0)
        col = lax.broadcasted_iota(jnp.int32, shape, 1)
        spos = (b - LEFT_MAX) * fr + col
        tpos = b * fr + row
        apart = LEFT_MAX - col // fr
        allowed = (spos >= 0) & (spos <= tpos) & (apart <= count)
        allowed = allowed & ((spos < length) | (spos == tpos))
        return attend_block(q1[at_rows(b, fr), :], k1[span, :], v1[span, :], allowed)

    def ahead(b):
        span = pl.ds(pl.multiple_of(b * fr, fr), 2 * fr)
        shape = (fr, 2 * fr)
        row = lax.broadcasted_iota(jnp.int32, shape, 0)
        col = lax.broadcasted_iota(jnp.int32, shape, 1)
        spos = b * fr + col
        allowed = (col <= row + RIGHT) & ((spos < length) | (col == row))
        out = attend_block(q2[at_rows(b, fr), :], k2[span, :], v2[span, :], allowed)
        valid = b * fr + lax.broadcasted_iota(jnp.int32, (fr, cols), 0) < length
        return jnp.where(valid, out, jnp.zeros_like(out))

    def turned_cols(which, index):
        return lax.rem(index - z * (rows // cols) + n, n) if which == 0 else index

    def back_copy(which, d):
        src, dst = ((ctx1s, ctx1), (ctx2s, ctx2))[which]
        b = lax.rem(t + d, n)
        return pltpu.make_async_remote_copy(
            src_ref=src.at[at_rows(b, fr), :],
            dst_ref=dst.at[:, at_cols(turned_cols(which, t))],
            send_sem=a2_send.at[which, d], recv_sem=a2_recv.at[which, d],
            device_id=(b, z), device_id_type=MESH,
        )

    def back_wait(which):
        src, dst = ((ctx1s, ctx1), (ctx2s, ctx2))[which]
        for d in range(1, n):
            b = lax.rem(t + n - d, n)
            pltpu.make_async_remote_copy(
                src_ref=src.at[at_rows(b, fr), :],
                dst_ref=dst.at[:, at_cols(turned_cols(which, b))],
                send_sem=a2_send.at[which, d], recv_sem=a2_recv.at[which, d],
                device_id=(b, z), device_id_type=MESH,
            ).wait_recv()

    def blocks(which, first, last):
        fun, src = ((causal, ctx1s), (ahead, ctx2s))[which]

        def body(d, carry):
            b = lax.rem(t + d, n)
            src[at_rows(b, fr), :] = fun(b)
            back_copy(which, d).start()
            return carry

        lax.fori_loop(first, last, body, 0)

    def own_block(which):
        fun, src, dst = ((causal, ctx1s, ctx1), (ahead, ctx2s, ctx2))[which]
        out = fun(t)
        src[at_rows(t, fr), :] = out
        dst[:, at_cols(turned_cols(which, t))] = out

    blocks(0, 1, n // 2)
    ag_forward(1, 2)
    chain(2, 1)
    blocks(0, n // 2, n)
    own_block(0)
    ag_forward(2, 0)
    ag_forward(2, 1)
    ag_forward(2, 2)
    ag_partner(2)
    back_wait(0)

    mixed = jnp.dot(ctx1[...], wo[...], preferred_element_type=jnp.float32)
    hidden = (frames_ref[...].astype(jnp.float32) + mixed).astype(jnp.bfloat16)
    nbuf2[t] = norm_rows(hidden, gain_two_ref[...])
    ag_start(3)
    for step in range(2, nz - 1):
        chain(2, step)
    ag_forward(3, 0)
    chain_end(2)
    ag_wait(3, 0)
    project(nbuf2, w2, q2, k2, v2, 0, t // 2)
    ag_forward(3, 1)
    ag_wait(3, 7)
    project(nbuf2, w2, q2, k2, v2, 0, flip(t, 2) // 2)
    ag_wait(3, 8)
    project(nbuf2, w2, q2, k2, v2, 0, flip(t, 4) // 2)
    ag_forward(3, 2)
    ag_wait(3, 9)
    ag_wait(3, 10)
    project(nbuf2, w2, q2, k2, v2, 0, flip(t, 6) // 2)
    blocks(1, 1, n)
    own_block(1)
    ag_partner(1)

    def term(zz):
        return jnp.dot(
            cott[at_rows(zz, rows), :], ctx2s[...], preferred_element_type=jnp.float32
        )

    def z_copy(d, back):
        to = lax.rem(z + d, nz)
        return pltpu.make_async_remote_copy(
            src_ref=gsend.at[d], dst_ref=grecv.at[d],
            send_sem=z_send.at[d], recv_sem=z_recv.at[d],
            device_id=(t, to), device_id_type=MESH,
        )

    for d in range(1, nz):
        gsend[d] = term(lax.rem(z + d, nz)).astype(jnp.bfloat16)
        z_copy(d, False).start()
    total = term(z)
    for d in range(1, nz):
        z_copy(d, True).wait_recv()
        total = total + grecv[d].astype(jnp.float32)
    gsum[...] = total

    def g_copy(d):
        b = lax.rem(t + d, n)
        return pltpu.make_async_remote_copy(
            src_ref=gsum.at[at_rows(b, part), :],
            dst_ref=wgr.at[:, pl.ds(mine, cols)],
            send_sem=a2_send.at[2, d], recv_sem=a2_recv.at[2, d],
            device_id=(b, z), device_id_type=MESH,
        )

    for d in range(1, n):
        g_copy(d).start()
    wgr[:, pl.ds(mine, cols)] = gsum[at_rows(t, part), :]
    back_wait(1)
    context_ref[...] = ctx2[...]
    for d in range(1, n):
        b = lax.rem(t + n - d, n)
        pltpu.make_async_remote_copy(
            src_ref=gsum.at[at_rows(b, part), :],
            dst_ref=wgr.at[:, at_cols(b)],
            send_sem=a2_send.at[2, d], recv_sem=a2_recv.at[2, d],
            device_id=(b, z), device_id_type=MESH,
        ).wait_recv()
    grad_ref[...] = wgr[...]
    for which in range(4):
        ag_sent(which)
    for which in range(3):
        chain_sent(which)
    for d in range(1, n):
        back_copy(0, d).wait_send()
        back_copy(1, d).wait_send()
        g_copy(d).wait_send()
    for d in range(1, nz):
        z_copy(d, False).wait_send()


def hand_out(context_ref, grad_ref, context_out, grad_out):
    context_out[...] = context_ref[...]
    grad_out[...] = grad_ref[...]


def by_heads(
    n, nz, frames, gain_one, qkv_one, out_one, gain_two, qkv_two, lengths, left_counts, cotangent
):
    _, fr, width = frames.shape
    cols = width // n
    rows = width // nz
    span = n * fr
    vmem = pl.BlockSpec(memory_space=pltpu.VMEM)
    smem = pl.BlockSpec(memory_space=pltpu.SMEM)
    hbm = pl.BlockSpec(memory_space=pl.ANY)
    bf16, f32 = jnp.bfloat16, jnp.float32
    dma = pltpu.SemaphoreType.DMA
    context, grad = pl.pallas_call(
        functools.partial(heads_kernel, n, nz),
        out_shape=(
            jax.ShapeDtypeStruct((fr, width), bf16),
            jax.ShapeDtypeStruct((rows // n, width), f32),
        ),
        in_specs=[vmem, vmem, hbm, hbm, vmem, hbm, smem, smem, hbm],
        out_specs=(vmem, vmem),
        scratch_shapes=[
            pltpu.VMEM((n, fr, width), bf16),
            pltpu.VMEM((n, fr, width), bf16),
            pltpu.VMEM((width, 3 * cols), bf16),
            pltpu.VMEM((width, 3 * cols), bf16),
            pltpu.VMEM((width, width), bf16),
            pltpu.VMEM((fr, width), bf16),
            pltpu.VMEM((width, span), bf16),
            pltpu.VMEM((span, cols), bf16),
            pltpu.VMEM((span + LEFT_MAX * fr, cols), bf16),
            pltpu.VMEM((span + LEFT_MAX * fr, cols), bf16),
            pltpu.VMEM((span, cols), bf16),
            pltpu.VMEM((fr, width), bf16),
            pltpu.VMEM((span, cols), bf16),
            pltpu.VMEM((span + fr, cols), bf16),
            pltpu.VMEM((span + fr, cols), bf16),
            pltpu.VMEM((span, cols), bf16),
            pltpu.VMEM((fr, width), bf16),
            pltpu.VMEM((nz, rows, cols), bf16),
            pltpu.VMEM((nz, rows, cols), bf16),
            pltpu.VMEM((rows, cols), f32),
            pltpu.VMEM((rows // n, width), f32),
            dma((8,)),
            dma((4, 11)),
            dma((4, 11)),
            dma((3, 2, nz, 2)),
            dma((3, nz, 2)),
            dma((3, n)),
            dma((3, n)),
            dma((nz,)),
            dma((nz,)),
        ],
        compiler_params=pltpu.CompilerParams(
            collective_id=0, has_side_effects=True, vmem_limit_bytes=60 * 1024 * 1024
        ),
    )(
        frames[0], gain_one[None], qkv_one, out_one, gain_two[None], qkv_two,
        lengths, left_counts, cotangent[0],
    )
    context, grad = pl.pallas_call(
        hand_out,
        out_shape=(
            jax.ShapeDtypeStruct((fr, width), bf16),
            jax.ShapeDtypeStruct((rows // n, width), f32),
        ),
        in_specs=[vmem, vmem],
        out_specs=(vmem, vmem),
    )(context, grad)
    return (context[None], grad)


def solution(mesh):
    n_tm = mesh.shape["tm"]
    even = n_tm == 2 * CHIPS and mesh.shape["fsdp"] == CHIPS and HEADS % n_tm == 0
    chosen = functools.partial(by_heads, n_tm, mesh.shape["fsdp"]) if even else on_device
    in_specs = (
        P("fsdp", "tm", None),
        P(),
        P("fsdp", None),
        P("fsdp", None),
        P(),
        P("fsdp", None),
        P("fsdp"),
        P("fsdp"),
        P("fsdp", "tm", None),
    )
    out_specs = (P("fsdp", "tm", None), P(("tm", "fsdp"), None))
    return jax.shard_map(
        chosen, mesh=mesh, in_specs=in_specs, out_specs=out_specs, check_vma=False
    )
```
